128 devices in a mesh: dp: 16 (over z, x), seq: 8 (over y, core).
Axes of the slice: x: 4, y: 4, z: 4, core: 2. Of those that a mesh axis runs over, the one named last changes fastest.
Arguments:
- layer_input: bfloat16 [2, 16, 1024, 896], P(None, 'dp', 'seq'), may hold values from -6 to 6
- pic_start: int32 [2, 16], P(None, 'dp'), may hold values from 0 to 768, as said below
- norm_one: bfloat16 [896], P('dp'), may hold values from 0.099609375 to 1.8984375
- w_query: bfloat16 [896, 896], P('dp'), may hold values from -0.1875 to 0.1875
- b_query: bfloat16 [896], P('dp'), may hold values from -3 to 3
- w_key: bfloat16 [896, 128], P('dp'), may hold values from -0.1875 to 0.1875
- b_key: bfloat16 [128], P('dp'), may hold values from -3 to 3
- w_value: bfloat16 [896, 128], P('dp'), may hold values from -0.1875 to 0.1875
- b_value: bfloat16 [128], P('dp'), may hold values from -3 to 3
- w_out: bfloat16 [896, 896], P('dp'), may hold values from -1.5 to 1.5
- norm_two: bfloat16 [896], P('dp'), may hold values from 0.099609375 to 1.8984375
- w_gate: bfloat16 [896, 4864], P('dp'), may hold values from -0.1875 to 0.1875
- w_up: bfloat16 [896, 4864], P('dp'), may hold values from -0.1875 to 0.1875
- w_down: bfloat16 [4864, 896], P('dp'), may hold values from -0.078125 to 0.078125
- out_grad: bfloat16 [2, 16, 1024, 896], P(None, 'dp', 'seq'), may hold values from -6 to 6
Outputs:
- layer_output: bfloat16 [2, 16, 1024, 896], P(None, 'dp', 'seq')
- input_grad: float32 [2, 16, 1024, 896], P(None, 'dp', 'seq')
- norm_one_grad: float32 [896], P('dp')
- w_query_grad: float32 [896, 896], P('dp')
- b_query_grad: float32 [896], P('dp')
- w_key_grad: float32 [896, 128], P('dp')
- b_key_grad: float32 [128], P('dp')
- w_value_grad: float32 [896, 128], P('dp')
- b_value_grad: float32 [128], P('dp')
- w_out_grad: float32 [896, 896], P('dp')
- norm_two_grad: float32 [896], P('dp')
- w_gate_grad: float32 [896, 4864], P('dp')
- w_up_grad: float32 [896, 4864], P('dp')
- w_down_grad: float32 [4864, 896], P('dp')
The draws below stay inside these ranges and needn't reach their ends.
Inputs may be any that keep to these rules, and one draw needn't show every extreme that they name: Each sequence has one picture block of 256 tokens starting at its pic_start, a multiple of 256.
All inputs are finite; a program needn't handle non-finite values.
Results may differ from the reference program's by a relative error of at most 0.028.
Values may be sent and summed in bfloat16 or wider, within the bound.
A program may use at most 192 MiB of HBM per device.

```python
import jax
import jax.numpy as jnp
from jax import lax

D = 896
HEADS = 14
KV_HEADS = 2
HD = 64
FF = 4864
SEQ_LEN = 1024
PIC = 256
MB = 2
SEQS = 16


def draw_pic_start(key, part):
    blocks = SEQ_LEN // PIC
    picked = jax.random.randint(key, (MB, SEQS), 0, blocks)
    picked = picked.at[0, 0].set(0).at[0, 1].set(blocks - 1)
    return (picked * PIC).astype(jnp.int32)


def shard_levels(own_key, dims, shards, smallest, largest):
    loudness = 1.0
    for dim, shards_of in shards:
        draws = jax.random.uniform(jax.random.fold_in(jax.random.fold_in(own_key, 6), dim), (shards_of,), jnp.float32, smallest / len(shards), largest / len(shards))
        loudness = loudness * jnp.repeat(jnp.exp(draws), dims[dim] // shards_of).reshape((-1,) + (1,) * (len(dims) - 1 - dim))
    return loudness


def normal_values(key, extent, scale, reach, split=(), kind=jnp.bfloat16):
    values = jax.random.normal(key, extent, jnp.float32) * scale
    if len(split) > 0:
        values = shard_levels(key, extent, split, -0.22, 0.18) * values
    return jnp.clip(values, min=-reach, max=reach).astype(kind)


def setup_inputs(seed: int = 0) -> dict:
    key_list = jax.random.split(jax.random.key(seed), 16)
    return {
        "layer_input": normal_values(key_list[0], (MB, SEQS, SEQ_LEN, D), 1.0, 6.0, ((1, 16), (2, 8))),
        "pic_start": draw_pic_start(jax.random.fold_in(key_list[15], 71), 0),
        "norm_one": jnp.clip(1.0 + 0.18 * jax.random.normal(key_list[2], (D,), jnp.float32), 0.099609375, 1.8984375).astype(jnp.bfloat16),
        "w_query": normal_values(key_list[3], (D, HEADS * HD), D ** -0.5, 0.1875, ((0, 16),)),
        "b_query": normal_values(key_list[4], (HEADS * HD,), 0.5, 3.0, ((0, 16),)),
        "w_key": normal_values(key_list[5], (D, KV_HEADS * HD), D ** -0.5, 0.1875, ((0, 16),)),
        "b_key": normal_values(key_list[6], (KV_HEADS * HD,), 0.5, 3.0, ((0, 16),)),
        "w_value": normal_values(key_list[7], (D, KV_HEADS * HD), D ** -0.5, 0.1875, ((0, 16),)),
        "b_value": normal_values(key_list[8], (KV_HEADS * HD,), 0.5, 3.0, ((0, 16),)),
        "w_out": normal_values(key_list[9], (HEADS * HD, D), (D // 64) ** -0.5, 1.5, ((0, 16),)),
        "norm_two": jnp.clip(1.0 + 0.18 * jax.random.normal(key_list[10], (D,), jnp.float32), 0.099609375, 1.8984375).astype(jnp.bfloat16),
        "w_gate": normal_values(key_list[11], (D, FF), D ** -0.5, 0.1875, ((0, 16),)),
        "w_up": normal_values(key_list[12], (D, FF), D ** -0.5, 0.1875, ((0, 16),)),
        "w_down": normal_values(key_list[13], (FF, D), FF ** -0.5, 0.078125, ((0, 16),)),
        "out_grad": normal_values(key_list[14], (MB, SEQS, SEQ_LEN, D), 1.0, 6.0, ((1, 16), (2, 8))),
    }


EPSILON = 1e-06
ROPE_BASE = 1000000.0
NEGATIVE = -1e+30
HIGHEST = lax.Precision.HIGHEST

@jax.custom_vjp
def low(v):
    return lax.optimization_barrier(v.astype(jnp.bfloat16)).astype(jnp.float32)

@jax.custom_vjp
def low_back(v):
    return v

def low_keep(v):
    return (low(v), None)

def low_pass(kept, grad):
    return (grad,)

def back_keep(v):
    return (v, None)

def back_low(kept, grad):
    return (low(grad),)
low.defvjp(low_keep, low_pass)
low_back.defvjp(back_keep, back_low)

def rope_tables(positions, head_dim):
    half_dim = head_dim // 2
    exponent = jnp.arange(half_dim, dtype=jnp.float32) * (2.0 / head_dim)
    inverse = ROPE_BASE ** (-exponent)
    angles = positions.astype(jnp.float32)[:, None] * inverse[None, :]
    angles = jnp.concatenate([angles, angles], axis=1)
    return (jnp.cos(angles), jnp.sin(angles))

def rotate_half(inputs, head_dim):
    shaped = inputs.reshape(inputs.shape[:-1] + (inputs.shape[-1] // head_dim, 2, head_dim // 2))
    turned = jnp.stack([-shaped[..., 1, :], shaped[..., 0, :]], axis=-2)
    return turned.reshape(inputs.shape)

def rotate(inputs, cosine, sine, head_dim, direction):
    count = inputs.shape[-1] // head_dim
    cos_all = jnp.tile(cosine, (1, count))
    sin_all = jnp.tile(sine, (1, count))
    return inputs * cos_all + direction * rotate_half(inputs, head_dim) * sin_all

def visible_mask(query_pos, key_pos, start):
    inside_query = (query_pos >= start) & (query_pos < start + PIC)
    inside_key = (key_pos >= start) & (key_pos < start + PIC)
    return (key_pos[None, :] <= query_pos[:, None]) | inside_query[:, None] & inside_key[None, :]

def one_sequence(inputs, start, params):
    norm_gain, w_query, b_query, w_key, b_key, w_value, b_value, w_out, norm_gain_two, w_gate, w_up, w_down = params
    length = inputs.shape[0]
    group = HEADS // KV_HEADS
    positions = jnp.arange(length, dtype=jnp.int32)
    cosine, sine = rope_tables(positions, HD)
    inv_one = lax.rsqrt(lax.optimization_barrier(jnp.mean(inputs * inputs, axis=-1, keepdims=True)) + EPSILON)
    normed = low(inputs * inv_one * norm_gain)
    queries = low(rotate(low_back(jnp.dot(normed, w_query, precision=HIGHEST) + b_query), cosine, sine, HD, 1.0))
    keys = low(rotate(low_back(jnp.dot(normed, w_key, precision=HIGHEST) + b_key), cosine, sine, HD, 1.0))
    values = low(low_back(jnp.dot(normed, w_value, precision=HIGHEST) + b_value))
    query_heads = queries.reshape(length, KV_HEADS, group, HD)
    key_heads = keys.reshape(length, KV_HEADS, HD)
    value_heads = values.reshape(length, KV_HEADS, HD)
    scores = jnp.einsum('rkgd,lkd->kgrl', query_heads, key_heads, precision=HIGHEST) * HD ** (-0.5)
    scores = low_back(scores)
    masked = jnp.where(visible_mask(positions, positions, start), scores, NEGATIVE)
    row_max = lax.optimization_barrier(jnp.max(masked, axis=-1, keepdims=True))
    unnormed = jnp.exp(masked - row_max)
    probs = low(unnormed / lax.optimization_barrier(jnp.sum(unnormed, axis=-1, keepdims=True)))
    attended = jnp.einsum('kgrl,lkd->rkgd', probs, value_heads, precision=HIGHEST).reshape(length, HEADS * HD)
    attended = low_back(low(attended))
    resid = inputs + low_back(jnp.dot(attended, w_out, precision=HIGHEST))
    inv_two = lax.rsqrt(lax.optimization_barrier(jnp.mean(resid * resid, axis=-1, keepdims=True)) + EPSILON)
    normed_two = low(resid * inv_two * norm_gain_two)
    gate = low_back(low(jnp.dot(normed_two, w_gate, precision=HIGHEST)))
    upper = low_back(low(jnp.dot(normed_two, w_up, precision=HIGHEST)))
    hidden = low(low_back(gate * jax.nn.sigmoid(gate) * upper))
    return resid + low_back(jnp.dot(hidden, w_down, precision=HIGHEST))

def reference(layer_input, pic_start, norm_one, w_query, b_query, w_key, b_key, w_value, b_value, w_out, norm_two, w_gate, w_up, w_down, out_grad):
    params = tuple((p.astype(jnp.float32) for p in (norm_one, w_query, b_query, w_key, b_key, w_value, b_value, w_out, norm_two, w_gate, w_up, w_down)))
    inputs = layer_input.astype(jnp.float32).reshape(MB * SEQS, SEQ_LEN, D)
    starts = pic_start.reshape(MB * SEQS).astype(jnp.int32)

    def forward(inputs, params):

        def step(carry, element):
            return (carry, jax.checkpoint(one_sequence)(element[0], element[1], params))
        return lax.scan(step, jnp.zeros((), jnp.float32), (inputs, starts))[1]
    outputs, pullback = jax.vjp(forward, inputs, params)
    grad_inputs, grads = pullback(out_grad.astype(jnp.float32).reshape(MB * SEQS, SEQ_LEN, D))
    return (outputs.astype(jnp.bfloat16).reshape(MB, SEQS, SEQ_LEN, D), grad_inputs.reshape(MB, SEQS, SEQ_LEN, D), grads[0], grads[1], grads[2], grads[3], grads[4], grads[5], grads[6], grads[7], grads[8], grads[9], grads[10], grads[11])
```

```python
import functools

import jax
import jax.numpy as jnp
import numpy as np
from jax import lax
from jax.experimental import pallas as pl
from jax.experimental.pallas import tpu as pltpu
from jax.sharding import PartitionSpec as P

HEADS = 14
KV_HEADS = 2
HD = 64
PIC = 256
D = 896
FF = 4864
ROWS = 256
LANE = 128
SHARD = 56
FFS = 1280
DROWS = 304
DHALF = 152
QKV = 1152
PACK = 2304
EPSILON = 1e-06
ROPE_BASE = 1000000.0
NEGATIVE = -1e30
MESH = pl.DeviceIdType.MESH
BF = jnp.bfloat16
F32 = jnp.float32
VLIM = 60 * 1024 * 1024
UNIT0 = (0, 9, 19, 28)


def place():
    dp = lax.axis_index("dp")
    seq = lax.axis_index("seq")
    return dp // 4, dp % 4, seq // 2, seq % 2


def at(z, x, y, c):
    return ((z % 4) * 4 + x % 4, (y % 4) * 2 + c % 2)


def peers_of(axis):
    z, x, y, c = place()
    moves = (1, 3, 2)
    if axis == "z":
        return [at(z + m, x, y, c) for m in moves]
    if axis == "x":
        return [at(z, x + m, y, c) for m in moves]
    if axis == "y":
        return [at(z, x, y + m, c) for m in moves]
    return [at(z, x, y, c + 1)]


def greet(axes):
    barrier = pltpu.get_barrier_semaphore()
    count = 0
    for axis in axes:
        for peer in peers_of(axis):
            pl.semaphore_signal(barrier, inc=1, device_id=peer, device_id_type=MESH)
            count += 1
    pl.semaphore_wait(barrier, count)


def remote(src, dst, send, recv, peer):
    return pltpu.make_async_remote_copy(
        src_ref=src, dst_ref=dst, send_sem=send, recv_sem=recv, device_id=peer, device_id_type=MESH
    )


def start(copies):
    for copy in copies:
        copy.start()


def wait_recv(copies):
    for copy in copies:
        copy.wait_recv()


def wait_send(copies):
    for copy in copies:
        copy.wait_send()


def ring_copies(src, dst, ss, rs, axis):
    return [remote(src, dst, ss.at[k], rs.at[k], peer) for k, peer in enumerate(peers_of(axis))]


def outer_sum(left, right):
    return jnp.einsum("ta,tb->ab", left, right, preferred_element_type=F32)


def back_dot(grad_rows, weight):
    return jnp.einsum("tb,ab->ta", grad_rows, weight, preferred_element_type=F32)


def gather_kernel(
    p_ref, wg_ref, wu_ref, wd_ref, g_ref,
    p4, w4, wd, ga,
    zero, loc, ss, rs, dss, drs,
):
    z, x, y, c = place()
    greet(("z", "x", "y", "c"))
    zero[...] = jnp.zeros_like(zero)
    first = pl.multiple_of(((19 * y) // 2) * LANE, LANE)
    off = 64 * (y % 2)

    def down_rows(xx, cc):
        return pl.ds(pl.multiple_of(off + DROWS * xx + DHALF * cc, 8), DHALF)

    base = c * QKV
    mine = pl.ds(pl.multiple_of(base, LANE), QKV)
    locals_ = [
        pltpu.make_async_copy(p_ref.at[:, mine], p4.at[z, x, :, mine], loc.at[0]),
        pltpu.make_async_copy(g_ref, ga.at[y], loc.at[1]),
        pltpu.make_async_copy(
            zero, wd.at[pl.ds(pl.multiple_of(1216 * (1 - y % 2), 8), 64)], loc.at[2]
        ),
    ]
    start(locals_)
    own_w = [
        pltpu.make_async_copy(ref.at[:, pl.ds(first, FFS)], w4.at[c, z, x], loc.at[3])
        for ref in (wg_ref, wu_ref)
    ]

    @pl.when(c == 0)
    def _():
        own_w[0].start()

    @pl.when(c == 1)
    def _():
        own_w[1].start()

    cols_a = pl.ds(pl.multiple_of(base, LANE), 640)
    cols_b = pl.ds(pl.multiple_of(base + 640, LANE), 512)
    pa1 = ring_copies(p_ref.at[:, cols_a], p4.at[z, x, :, cols_a], ss.at[0], rs.at[0], "x")
    pb1 = ring_copies(p_ref.at[:, cols_b], p4.at[z, x, :, cols_b], ss.at[1], rs.at[1], "z")
    start(pa1)
    start(pb1)
    half = [pl.ds(0, 640), pl.ds(640, 640)]
    wa1 = ring_copies(w4.at[c, z, x, :, half[0]], w4.at[c, z, x, :, half[0]], ss.at[2], rs.at[2], "x")
    wb1 = ring_copies(w4.at[c, z, x, :, half[1]], w4.at[c, z, x, :, half[1]], ss.at[3], rs.at[3], "z")
    for copy in locals_ + own_w[:1]:
        copy.wait()
    start(wa1)
    start(wb1)
    own = down_rows(x, c)
    own_src = pl.ds(pl.multiple_of(DHALF * c, 8), DHALF)
    dz = [
        remote(wd_ref.at[own_src], wd.at[own], dss.at[k], drs.at[0], peer)
        for k, peer in enumerate(peers_of("z"))
    ]
    dloc = pltpu.make_async_copy(wd_ref.at[own_src], wd.at[own], loc.at[5])

    @pl.when(z == y)
    def _():
        dloc.start()
        start(dz)

    gy = ring_copies(g_ref, ga.at[y], ss.at[8], rs.at[8], "y")
    start(gy)

    pa2 = ring_copies(p4.at[z, :, :, cols_a], p4.at[z, :, :, cols_a], ss.at[4], rs.at[4], "z")
    pb2 = ring_copies(p4.at[:, x, :, cols_b], p4.at[:, x, :, cols_b], ss.at[5], rs.at[5], "x")
    wa2 = ring_copies(w4.at[c, z, :, :, half[0]], w4.at[c, z, :, :, half[0]], ss.at[6], rs.at[6], "z")
    wb2 = ring_copies(w4.at[c, :, x, :, half[1]], w4.at[c, :, x, :, half[1]], ss.at[7], rs.at[7], "x")
    wait_recv(pa1)
    start(pa2)
    wait_recv(pb1)
    start(pb2)
    wait_recv(wa1)
    start(wa2)
    wait_recv(wb1)
    start(wb2)

    @pl.when(z == y)
    def _():
        dloc.wait()

    @pl.when(z != y)
    def _():
        dz[0].wait_recv()

    dx = ring_copies(wd.at[own], wd.at[own], dss.at[pl.ds(3, 3)], drs.at[pl.ds(1, 3)], "x")
    start(dx)
    sibling = peers_of("c")[0]
    wait_recv(pa2)
    wait_recv(pb2)
    psib = remote(p4.at[:, :, :, mine], p4.at[:, :, :, mine], dss.at[6], drs.at[4], sibling)
    psib.start()
    wait_recv(wa2)
    wait_recv(wb2)
    wsib = remote(w4.at[c], w4.at[c], dss.at[7], drs.at[5], sibling)
    wsib.start()
    wait_recv(dx)
    dsib = [
        remote(wd.at[down_rows(xx, c)], wd.at[down_rows(xx, c)], dss.at[8 + xx], drs.at[6 + xx], sibling)
        for xx in range(4)
    ]
    start(dsib)
    wait_recv(gy)
    psib.wait_recv()
    wsib.wait_recv()
    wait_recv(dsib)

    @pl.when(z == y)
    def _():
        wait_send(dz)

    for group in (pa1, pb1, wa1, wb1, pa2, pb2, wa2, wb2, gy, dx, [psib], [wsib], dsib):
        wait_send(group)


def gather_all(pack, w_gate, w_up, w_down, grads):
    anyspec = pl.BlockSpec(memory_space=pl.ANY)
    return pl.pallas_call(
        gather_kernel,
        out_shape=(
            jax.ShapeDtypeStruct((4, 4, SHARD, PACK), BF),
            jax.ShapeDtypeStruct((2, 4, 4, SHARD, FFS), BF),
            jax.ShapeDtypeStruct((FFS, D), BF),
            jax.ShapeDtypeStruct((4, ROWS, D), BF),
        ),
        in_specs=[anyspec] * 5,
        out_specs=(anyspec,) * 4,
        scratch_shapes=[
            pltpu.VMEM((64, D), BF),
            pltpu.SemaphoreType.DMA((6,)),
            pltpu.SemaphoreType.DMA((9, 3)),
            pltpu.SemaphoreType.DMA((9, 3)),
            pltpu.SemaphoreType.DMA((12,)),
            pltpu.SemaphoreType.DMA((10,)),
        ],
        compiler_params=pltpu.CompilerParams(
            collective_id=0, has_side_effects=True, vmem_limit_bytes=VLIM
        ),
        name="gather_weights",
    )(pack, w_gate, w_up, w_down, grads)


def mlp_kernel(
    x_ref, ga_ref, w_ref, wd_ref, resid_ref,
    out_ref, ng_ref, dw_ref, dwd_ref,
    xall, hid, gg, ug, outp, ngp, outr, ngr, xt, acc_out, ss, rs,
):
    z, x, y, c = place()
    greet(("y",))
    xall[y] = x_ref[...]
    xs = ring_copies(xall.at[y], xall.at[y], ss.at[0], rs.at[0], "y")
    start(xs)

    def hop(k):
        return jnp.where(k == 1, 3, jnp.where(k == 2, 1, jnp.where(k == 3, 2, 0)))

    def send_back(buf, dst, k, group):
        yk = y + hop(k)
        return remote(
            buf.at[k], dst.at[jnp.maximum(k - 1, 0)], ss.at[group, jnp.maximum(k - 1, 0)],
            rs.at[group, jnp.maximum(k - 1, 0)], at(z, x, yk, c),
        )

    def block(k, carry):
        yk = (y + hop(k)) % 4

        @pl.when(k > 0)
        def _():
            index = jnp.maximum(k - 1, 0)
            remote(
                xall.at[y], xall.at[y], ss.at[0, index], rs.at[0, index], at(z, x, y + 1, c)
            ).wait_recv()

        rows = pl.ds(pl.multiple_of(k * ROWS, ROWS), ROWS)

        def tile(n, carry):
            cols = pl.ds(pl.multiple_of(n * 256, 256), 256)
            xb = xall[yk]
            gb = ga_ref[yk]
            gate = jnp.dot(xb, w_ref[0, :, cols], preferred_element_type=F32).astype(BF).astype(F32)
            up = jnp.dot(xb, w_ref[1, :, cols], preferred_element_type=F32).astype(BF).astype(F32)
            hg = lax.dot_general(
                gb, wd_ref[cols, :], (((1,), (1,)), ((), ())), preferred_element_type=F32
            ).astype(BF).astype(F32)
            sig = jax.nn.sigmoid(gate)
            act = gate * sig
            hid[rows, cols] = (act * up).astype(BF)
            ug[rows, cols] = (hg * act).astype(BF)
            gg[rows, cols] = (hg * up * sig * (1.0 + gate * (1.0 - sig))).astype(BF)
            return carry

        lax.fori_loop(0, 5, tile, 0)
        ngp_f = lax.dot_general(
            gg[rows, :], w_ref[0], (((1,), (1,)), ((), ())), preferred_element_type=F32
        ) + lax.dot_general(
            ug[rows, :], w_ref[1], (((1,), (1,)), ((), ())), preferred_element_type=F32
        )

        @pl.when(k == 0)
        def _():
            ng_ref[...] = ngp_f

        @pl.when(k > 0)
        def _():
            ngp[k] = ngp_f.astype(BF)
            send_back(ngp, ngr, k, 1).start()

        out_f = jnp.dot(hid[rows, :], wd_ref[...], preferred_element_type=F32)

        @pl.when(k == 0)
        def _():
            acc_out[...] = resid_ref[...] + out_f

        @pl.when(k > 0)
        def _():
            outp[k] = out_f.astype(BF)
            send_back(outp, outr, k, 2).start()

        xt[:, rows] = xall[yk].T
        return carry

    lax.fori_loop(0, 4, block, 0)

    def wtile(n, carry):
        cols = pl.ds(pl.multiple_of(n * 256, 256), 256)
        dw_ref[0, :, cols] = jnp.dot(xt[...], gg[:, cols], preferred_element_type=F32).astype(BF)
        dw_ref[1, :, cols] = jnp.dot(xt[...], ug[:, cols], preferred_element_type=F32).astype(BF)
        acc = jnp.zeros((256, D), F32)
        for k in range(4):
            yk = (y + (0, 3, 1, 2)[k]) % 4
            acc += lax.dot_general(
                hid[pl.ds(k * ROWS, ROWS), cols], ga_ref[yk], (((0,), (0,)), ((), ())),
                preferred_element_type=F32,
            )
        dwd_ref[cols, :] = acc.astype(BF)
        return carry

    lax.fori_loop(0, 5, wtile, 0)
    for k in (1, 2, 3):
        send_back(ngp, ngr, k, 1).wait_recv()
    ng_ref[...] = (
        ng_ref[...] + ngr[0].astype(F32) + ngr[1].astype(F32) + ngr[2].astype(F32)
    )
    for k in (1, 2, 3):
        send_back(outp, outr, k, 2).wait_recv()
    out_ref[...] = (
        acc_out[...] + outr[0].astype(F32) + outr[1].astype(F32) + outr[2].astype(F32)
    ).astype(BF)
    wait_send(xs)
    for k in (1, 2, 3):
        send_back(ngp, ngr, k, 1).wait_send()
        send_back(outp, outr, k, 2).wait_send()


def feed_forward(normed_two, ga, w2, wd, resid):
    vm = pl.BlockSpec(memory_space=pltpu.VMEM)
    return pl.pallas_call(
        mlp_kernel,
        out_shape=(
            jax.ShapeDtypeStruct((ROWS, D), BF),
            jax.ShapeDtypeStruct((ROWS, D), F32),
            jax.ShapeDtypeStruct((2, D, FFS), BF),
            jax.ShapeDtypeStruct((FFS, D), BF),
        ),
        in_specs=[vm] * 5,
        out_specs=(vm,) * 4,
        scratch_shapes=[
            pltpu.VMEM((4, ROWS, D), BF),
            pltpu.VMEM((4 * ROWS, FFS), BF),
            pltpu.VMEM((4 * ROWS, FFS), BF),
            pltpu.VMEM((4 * ROWS, FFS), BF),
            pltpu.VMEM((4, ROWS, D), BF),
            pltpu.VMEM((4, ROWS, D), BF),
            pltpu.VMEM((3, ROWS, D), BF),
            pltpu.VMEM((3, ROWS, D), BF),
            pltpu.VMEM((D, 4 * ROWS), BF),
            pltpu.VMEM((ROWS, D), F32),
            pltpu.SemaphoreType.DMA((3, 3)),
            pltpu.SemaphoreType.DMA((3, 3)),
        ],
        compiler_params=pltpu.CompilerParams(
            collective_id=1, has_side_effects=True, vmem_limit_bytes=VLIM
        ),
        name="feed_forward",
    )(normed_two, ga, w2, wd, resid)


def total(parts):
    acc = parts[0].astype(F32)
    for part in parts[1:]:
        acc = acc + part.astype(F32)
    return acc


def reduce_kernel(
    da_ref, dw_ref, dd_ref,
    oa_ref, og_ref, ou_ref, od_ref,
    ma, sa, mw, sw, md, sd,
    ra1, rb1, ba1, bb1, ra2, rb2, ya, fsib,
    wra1, wrb1, wba1, wbb1, wra2, wrb2, yw,
    dr1, db1, dr2, fin,
    loc, sib_s, sib_r, ss, rs, xs_, xr_,
):
    z, x, y, c = place()
    greet(("z", "x", "y", "c"))
    sibling = peers_of("c")[0]
    off = 64 * (y % 2)

    def cols_of(cc):
        return pl.ds(pl.multiple_of(cc * QKV, LANE), QKV)

    def down_rows(xx, cc):
        return pl.ds(pl.multiple_of(off + DROWS * xx + DHALF * cc, 8), DHALF)

    other = 1 - c
    to_sib = [
        remote(da_ref.at[:, :, :, cols_of(other)], sa, sib_s.at[0], sib_r.at[0], sibling),
        remote(dw_ref.at[other], sw, sib_s.at[1], sib_r.at[1], sibling),
    ] + [
        remote(dd_ref.at[down_rows(xx, other)], sd.at[xx], sib_s.at[2 + xx], sib_r.at[2 + xx], sibling)
        for xx in range(4)
    ]
    start(to_sib)
    local = [
        pltpu.make_async_copy(da_ref.at[:, :, :, cols_of(c)], ma, loc.at[0]),
        pltpu.make_async_copy(dw_ref.at[c], mw, loc.at[1]),
    ] + [
        pltpu.make_async_copy(dd_ref.at[down_rows(xx, c)], md.at[xx], loc.at[2 + xx])
        for xx in range(4)
    ]
    start(local)
    moves = (1, 3, 2)
    a_cols, b_cols = pl.ds(0, 640), pl.ds(640, 512)
    w_cols = (pl.ds(0, 640), pl.ds(640, 640))
    px, pz, py = peers_of("x"), peers_of("z"), peers_of("y")

    def merge(mine, theirs):
        def body(i, carry):
            zz, xx = i // 4, i % 4
            mine[zz, xx] = (mine[zz, xx].astype(F32) + theirs[zz, xx].astype(F32)).astype(BF)
            return carry

        lax.fori_loop(0, 16, body, 0)

    def first_x(mine, cols, dst, j):
        return [
            remote(mine.at[:, (x + m) % 4, :, cols], dst.at[k], ss.at[j, k], rs.at[j, k], px[k])
            for k, m in enumerate(moves)
        ]

    def first_z(mine, cols, dst, j):
        return [
            remote(mine.at[(z + m) % 4, :, :, cols], dst.at[k], ss.at[j, k], rs.at[j, k], pz[k])
            for k, m in enumerate(moves)
        ]

    def second(buf, index, peers, dst, j):
        return [
            remote(buf.at[(index + m) % 4], dst.at[k], ss.at[j, k], rs.at[j, k], peers[k])
            for k, m in enumerate(moves)
        ]

    local[0].wait()
    to_sib[0].wait_recv()
    merge(ma, sa)
    a1 = first_x(ma, a_cols, ra1, 0)
    b1 = first_z(ma, b_cols, rb1, 1)
    start(a1)
    start(b1)
    local[1].wait()
    to_sib[1].wait_recv()
    merge(mw, sw)
    wa1 = first_x(mw, w_cols[0], wra1, 2)
    wb1 = first_z(mw, w_cols[1], wrb1, 3)
    start(wa1)
    start(wb1)
    for xx in range(4):
        local[2 + xx].wait()
        to_sib[2 + xx].wait_recv()

    def merge_down(i, carry):
        md[i] = (md[i].astype(F32) + sd[i].astype(F32)).astype(BF)
        return carry

    lax.fori_loop(0, 4, merge_down, 0)
    d1 = [
        remote(md.at[(x + m) % 4], dr1.at[k], ss.at[4, k], rs.at[4, k], px[k])
        for k, m in enumerate(moves)
    ]
    start(d1)

    def sum_first(mine_of, recv, buf):
        def body(i, carry):
            buf[i] = total([mine_of(i), recv[0, i], recv[1, i], recv[2, i]]).astype(BF)
            return carry

        lax.fori_loop(0, 4, body, 0)

    wait_recv(a1)
    sum_first(lambda i: ma[i, x, :, a_cols], ra1, ba1)
    a2 = second(ba1, z, pz, ra2, 5)
    start(a2)
    wait_recv(b1)
    sum_first(lambda i: ma[z, i, :, b_cols], rb1, bb1)
    b2 = second(bb1, x, px, rb2, 6)
    start(b2)
    wait_recv(wa1)
    sum_first(lambda i: mw[i, x, :, w_cols[0]], wra1, wba1)
    wa2 = second(wba1, z, pz, wra2, 7)
    start(wa2)
    wait_recv(wb1)
    sum_first(lambda i: mw[z, i, :, w_cols[1]], wrb1, wbb1)
    wb2 = second(wbb1, x, px, wrb2, 8)
    start(wb2)
    wait_recv(d1)
    db1[...] = total([md[x], dr1[0], dr1[1], dr1[2]]).astype(BF)
    slot = (z - y + 3) % 4
    dz = remote(
        db1, dr2.at[jnp.minimum(slot, 2)], xs_.at[0], xr_.at[jnp.minimum(slot, 2)], at(y, x, y, c)
    )

    @pl.when(z != y)
    def _():
        dz.start()

    wait_recv(a2)
    ya[y, :, a_cols] = total([ba1[z], ra2[0], ra2[1], ra2[2]]).astype(BF)
    wait_recv(b2)
    ya[y, :, b_cols] = total([bb1[x], rb2[0], rb2[1], rb2[2]]).astype(BF)
    y1 = ring_copies(ya.at[y], ya.at[y], ss.at[9], rs.at[9], "y")
    start(y1)
    wait_recv(wa2)
    yw[c, y, :, w_cols[0]] = total([wba1[z], wra2[0], wra2[1], wra2[2]]).astype(BF)
    wait_recv(wb2)
    yw[c, y, :, w_cols[1]] = total([wbb1[x], wrb2[0], wrb2[1], wrb2[2]]).astype(BF)
    y2 = ring_copies(yw.at[c, y], yw.at[c, y], ss.at[10], rs.at[10], "y")
    start(y2)
    dy = [
        remote(fin.at[c], fin.at[c], xs_.at[1 + k], xr_.at[3], peer) for k, peer in enumerate(py)
    ]

    @pl.when(z == y)
    def _():
        for k in range(3):
            remote(db1, dr2.at[k], xs_.at[0], xr_.at[k], at(y, x, y, c)).wait_recv()
        fin[c] = total([db1[...], dr2[0], dr2[1], dr2[2]]).astype(BF)
        start(dy)

    wait_recv(y1)
    fsib[c] = total([ya[0], ya[1], ya[2], ya[3]])
    fs = remote(fsib.at[c], fsib.at[c], sib_s.at[6], sib_r.at[6], sibling)
    fs.start()
    wait_recv(y2)
    ws = remote(yw.at[c], yw.at[c], sib_s.at[7], sib_r.at[7], sibling)
    ws.start()

    @pl.when(z != y)
    def _():
        dy[0].wait_recv()

    ds_ = remote(fin.at[c], fin.at[c], sib_s.at[8], sib_r.at[8], sibling)
    ds_.start()
    fs.wait_recv()
    oa_ref[:, 0:QKV] = fsib[0]
    oa_ref[:, QKV:PACK] = fsib[1]
    ws.wait_recv()

    def spread(index, out):
        def piece(yy, lo, n):
            return yw[index, yy, :, lo * LANE : (lo + n) * LANE].astype(F32)

        def put(unit, value):
            out[:, unit * LANE : unit * LANE + value.shape[1]] = value

        put(0, piece(0, 0, 9))
        put(9, piece(0, 9, 1) + piece(1, 0, 1))
        put(10, piece(1, 1, 9))
        put(19, piece(2, 0, 9))
        put(28, piece(2, 9, 1) + piece(3, 0, 1))
        put(29, piece(3, 1, 9))

    spread(0, og_ref)
    spread(1, ou_ref)
    ds_.wait_recv()
    od_ref[0:DHALF] = fin[0].astype(F32)
    od_ref[DHALF:DROWS] = fin[1].astype(F32)

    @pl.when(z != y)
    def _():
        dz.wait_send()

    @pl.when(z == y)
    def _():
        wait_send(dy)

    for group in (to_sib, a1, b1, wa1, wb1, d1, a2, b2, wa2, wb2, y1, y2, [fs], [ws], [ds_]):
        wait_send(group)


def reduce_all(da, dw, dd):
    anyspec = pl.BlockSpec(memory_space=pl.ANY)
    vm = pl.BlockSpec(memory_space=pltpu.VMEM)
    v = lambda *shape: pltpu.VMEM(shape, BF)
    return pl.pallas_call(
        reduce_kernel,
        out_shape=(
            jax.ShapeDtypeStruct((SHARD, PACK), F32),
            jax.ShapeDtypeStruct((SHARD, FF), F32),
            jax.ShapeDtypeStruct((SHARD, FF), F32),
            jax.ShapeDtypeStruct((DROWS, D), F32),
        ),
        in_specs=[anyspec] * 3,
        out_specs=(vm,) * 4,
        scratch_shapes=[
            v(4, 4, SHARD, QKV), v(4, 4, SHARD, QKV),
            v(4, 4, SHARD, FFS), v(4, 4, SHARD, FFS),
            v(4, DHALF, D), v(4, DHALF, D),
            v(3, 4, SHARD, 640), v(3, 4, SHARD, 512), v(4, SHARD, 640), v(4, SHARD, 512),
            v(3, SHARD, 640), v(3, SHARD, 512), v(4, SHARD, QKV), pltpu.VMEM((2, SHARD, QKV), F32),
            v(3, 4, SHARD, 640), v(3, 4, SHARD, 640), v(4, SHARD, 640), v(4, SHARD, 640),
            v(3, SHARD, 640), v(3, SHARD, 640), v(2, 4, SHARD, FFS),
            v(3, DHALF, D), v(DHALF, D), v(3, DHALF, D), v(2, DHALF, D),
            pltpu.SemaphoreType.DMA((6,)),
            pltpu.SemaphoreType.DMA((9,)),
            pltpu.SemaphoreType.DMA((9,)),
            pltpu.SemaphoreType.DMA((11, 3)),
            pltpu.SemaphoreType.DMA((11, 3)),
            pltpu.SemaphoreType.DMA((4,)),
            pltpu.SemaphoreType.DMA((4,)),
        ],
        compiler_params=pltpu.CompilerParams(
            collective_id=2, has_side_effects=True, vmem_limit_bytes=VLIM
        ),
        name="reduce_grads",
    )(da, dw, dd)


def rope_tables(positions, head_dim):
    half_dim = head_dim // 2
    exponent = jnp.arange(half_dim, dtype=jnp.float32) * (2.0 / head_dim)
    inverse = ROPE_BASE ** (-exponent)
    angles = positions.astype(jnp.float32)[:, None] * inverse[None, :]
    angles = jnp.concatenate([angles, angles], axis=1)
    return (jnp.cos(angles), jnp.sin(angles))


def rotate_half(inputs, head_dim):
    shaped = inputs.reshape(inputs.shape[:-1] + (inputs.shape[-1] // head_dim, 2, head_dim // 2))
    turned = jnp.stack([-shaped[..., 1, :], shaped[..., 0, :]], axis=-2)
    return turned.reshape(inputs.shape)


def rotate(inputs, cosine, sine, head_dim, direction):
    count = inputs.shape[-1] // head_dim
    cos_all = jnp.tile(cosine, (1, count))
    sin_all = jnp.tile(sine, (1, count))
    return inputs * cos_all + direction * rotate_half(inputs, head_dim) * sin_all


def visible_mask(query_pos, key_pos, start):
    inside_query = (query_pos >= start) & (query_pos < start + PIC)
    inside_key = (key_pos >= start) & (key_pos < start + PIC)
    return (key_pos[None, :] <= query_pos[:, None]) | inside_query[:, None] & inside_key[None, :]


def norm_rows(inputs, gain_row):
    inverse = lax.rsqrt(jnp.mean(inputs * inputs, axis=-1, keepdims=True) + EPSILON)
    return (inverse, inputs * inverse * gain_row)


def norm_back(inputs, inverse, gain_row, grad_normed):
    scaled_in = inputs * inverse
    gain_grad = jnp.sum(grad_normed * scaled_in, axis=0)
    weighted = grad_normed * gain_row
    grad_in = inverse * weighted - scaled_in * inverse * jnp.mean(
        weighted * scaled_in, axis=-1, keepdims=True
    )
    return (grad_in, gain_grad)


def per_device(
    layer_input,
    pic_start,
    norm_one,
    w_query,
    b_query,
    w_key,
    b_key,
    w_value,
    b_value,
    w_out,
    norm_two,
    w_gate,
    w_up,
    w_down,
    out_grad,
):
    micro_count, seq_count, row_count, model_width = layer_input.shape
    length = row_count * lax.axis_size("seq")
    tokens = seq_count * row_count
    tokens2 = micro_count * tokens
    group = HEADS // KV_HEADS
    score_scale = HD ** (-0.5)
    query_pos = lax.axis_index("seq") * row_count + jnp.arange(row_count, dtype=jnp.int32)
    key_pos = jnp.arange(length, dtype=jnp.int32)
    cosine, sine = rope_tables(jnp.tile(query_pos, micro_count * seq_count), HD)

    def scores_of(query_heads, key_heads, start):
        scores = (
            jnp.einsum("rkgd,lkd->kgrl", query_heads, key_heads, preferred_element_type=jnp.float32)
            * score_scale
        )
        return jnp.where(visible_mask(query_pos, key_pos, start), scores, NEGATIVE)

    def attend_forward(element):
        q_seq, k_seq, v_seq, start = element
        query_heads = q_seq.reshape(row_count, KV_HEADS, group, HD)
        key_heads = k_seq.reshape(length, KV_HEADS, HD)
        value_heads = v_seq.reshape(length, KV_HEADS, HD)
        masked = scores_of(query_heads, key_heads, start)
        row_max = jnp.max(masked, axis=-1, keepdims=True)
        unnormed = jnp.exp(masked - row_max)
        row_total = jnp.sum(unnormed, axis=-1, keepdims=True)
        probs = (unnormed / row_total).astype(jnp.bfloat16)
        attended = jnp.einsum(
            "kgrl,lkd->rkgd", probs, value_heads, preferred_element_type=jnp.float32
        )
        return (
            attended.reshape(row_count, HEADS * HD).astype(jnp.bfloat16),
            row_max + jnp.log(row_total),
        )

    def attend_backward(element):
        q_seq, k_seq, v_seq, start, log_total, grad_seq = element
        query_heads = q_seq.reshape(row_count, KV_HEADS, group, HD)
        key_heads = k_seq.reshape(length, KV_HEADS, HD)
        value_heads = v_seq.reshape(length, KV_HEADS, HD)
        grad_heads = grad_seq.reshape(row_count, KV_HEADS, group, HD)
        probs = jnp.exp(scores_of(query_heads, key_heads, start) - log_total)
        rounded = probs.astype(jnp.bfloat16)
        prob_grad = jnp.einsum(
            "rkgd,lkd->kgrl", grad_heads, value_heads, preferred_element_type=jnp.float32
        )
        centre = jnp.sum(probs * prob_grad, axis=-1, keepdims=True)
        score_grad = (probs * (prob_grad - centre)).astype(jnp.bfloat16)
        query_grad = (
            jnp.einsum("kgrl,lkd->rkgd", score_grad, key_heads, preferred_element_type=jnp.float32)
            * score_scale
        )
        key_grad = (
            jnp.einsum(
                "kgrl,rkgd->lkd", score_grad, query_heads, preferred_element_type=jnp.float32
            )
            * score_scale
        )
        value_grad = jnp.einsum(
            "kgrl,rkgd->lkd", rounded, grad_heads, preferred_element_type=jnp.float32
        )
        return (
            query_grad.reshape(row_count, HEADS * HD),
            key_grad.reshape(length, KV_HEADS * HD),
            value_grad.reshape(length, KV_HEADS * HD),
        )


    pad8 = lambda v: jnp.pad(v, (0, SHARD - v.shape[0]))
    ext = jnp.stack([norm_one, norm_two, b_query, pad8(b_key), pad8(b_value)], axis=1)
    ext = jnp.pad(ext, ((0, 0), (0, 256 - 5)))
    pack = jnp.concatenate([w_query, w_key, w_value, w_out, ext], axis=1)
    grads_in = out_grad.reshape(tokens2, D)
    p4, w4, wd, ga = gather_all(pack, w_gate, w_up, w_down, grads_in)
    pf = p4.reshape(D, PACK)
    w2 = w4.reshape(2, D, FFS)
    extf = pf[:, 2048:2056].astype(F32)
    gain_one, gain_two, qbias = extf[:, 0], extf[:, 1], extf[:, 2]
    kbias = extf[:, 3].reshape(16, SHARD)[:, :8].reshape(128)
    vbias = extf[:, 4].reshape(16, SHARD)[:, :8].reshape(128)
    inputs = layer_input.reshape(tokens2, D).astype(F32)
    inv_one, normed_float = norm_rows(inputs, gain_one)
    normed = normed_float.astype(BF)
    qkv = jnp.dot(normed, pf[:, :QKV], preferred_element_type=F32)
    qkv = qkv + jnp.concatenate([qbias, kbias, vbias])
    queries = rotate(qkv[:, :D], cosine, sine, HD, 1.0).astype(BF)
    keys = rotate(qkv[:, D : D + 128], cosine, sine, HD, 1.0).astype(BF)
    values = qkv[:, D + 128 :].astype(BF)
    kv = jnp.concatenate([keys, values], axis=1).reshape(2, row_count, 256)
    kv_all = lax.all_gather(kv, "seq", axis=1, tiled=True)
    keys_all, values_all = kv_all[..., :128], kv_all[..., 128:]
    query_seqs = queries.reshape(2, row_count, D)
    starts = pic_start.reshape(2)
    attended, log_total = lax.map(attend_forward, (query_seqs, keys_all, values_all, starts))
    att_rows = attended.reshape(tokens2, D)
    w_out_full = pf[:, QKV : QKV + D]
    resid = inputs + jnp.dot(att_rows, w_out_full, preferred_element_type=F32)
    inv_two, normed_two_float = norm_rows(resid, gain_two)
    normed_two = normed_two_float.astype(BF)
    output, grad_normed_two, dw, dd = feed_forward(normed_two, ga, w2, wd, resid)
    grad_middle, gain_two_grad = norm_back(resid, inv_two, gain_two, grad_normed_two)
    resid_grad = grads_in.astype(F32) + grad_middle
    attn_grad_low = resid_grad.astype(BF)
    out_wgrad = outer_sum(att_rows, attn_grad_low)
    heads_grad = back_dot(attn_grad_low, w_out_full).astype(BF)
    query_grad, key_part, value_part = lax.map(
        attend_backward,
        (query_seqs, keys_all, values_all, starts, log_total, heads_grad.reshape(2, row_count, D)),
    )
    kv_part = jnp.concatenate([key_part, value_part], axis=2).astype(BF)
    kv_grad = lax.psum_scatter(kv_part, "seq", scatter_dimension=1, tiled=True)
    kv_grad = kv_grad.astype(F32).reshape(tokens2, 256)
    qlin_grad = rotate(query_grad.reshape(tokens2, D), cosine, sine, HD, -1.0).astype(BF)
    klin_grad = rotate(kv_grad[:, :128], cosine, sine, HD, -1.0).astype(BF)
    vlin_grad = kv_grad[:, 128:].astype(BF)
    lin_grad = jnp.concatenate([qlin_grad, klin_grad, vlin_grad], axis=1)
    grad_normed = back_dot(lin_grad, pf[:, :QKV])
    grad_first, gain_one_grad = norm_back(inputs, inv_one, gain_one, grad_normed)
    input_grad = (resid_grad + grad_first).reshape(micro_count, seq_count, row_count, D)
    qkv_wgrad = outer_sum(normed, lin_grad)
    bias_grad = jnp.sum(lin_grad.astype(F32), axis=0)
    spread = lambda v: jnp.pad(v.reshape(16, 8), ((0, 0), (0, SHARD - 8))).reshape(D)
    ext_grad = jnp.stack(
        [gain_one_grad, gain_two_grad, bias_grad[:D], spread(bias_grad[D : D + 128]), spread(bias_grad[D + 128 :])],
        axis=1,
    )
    ext_grad = jnp.pad(ext_grad, ((0, 0), (0, 256 - 5)))
    da = jnp.concatenate([qkv_wgrad, out_wgrad, ext_grad], axis=1).astype(BF)
    oa, og, ou, od = reduce_all(
        da.reshape(4, 4, SHARD, PACK), dw.reshape(2, 4, 4, SHARD, FFS), dd
    )
    return (
        output.reshape(micro_count, seq_count, row_count, D),
        input_grad,
        oa[:, 2048],
        oa[:, :D],
        oa[:, 2050],
        oa[:, D : D + 128],
        oa[:8, 2051],
        oa[:, D + 128 : QKV],
        oa[:8, 2052],
        oa[:, QKV : QKV + D],
        oa[:, 2049],
        og,
        ou,
        od,
    )


def solution(mesh):
    placed = (
        P(None, "dp", "seq", None),
        P(None, "dp"),
        P("dp"),
        P("dp", None),
        P("dp"),
        P("dp", None),
        P("dp"),
        P("dp", None),
        P("dp"),
        P("dp", None),
        P("dp"),
        P("dp", None),
        P("dp", None),
        P("dp", None),
        P(None, "dp", "seq", None),
    )
    return jax.shard_map(
        per_device,
        mesh=mesh,
        in_specs=placed,
        out_specs=(
            P(None, "dp", "seq", None),
            P(None, "dp", "seq", None),
            P("dp"),
            P("dp", None),
            P("dp"),
            P("dp", None),
            P("dp"),
            P("dp", None),
            P("dp"),
            P("dp", None),
            P("dp"),
            P("dp", None),
            P("dp", None),
            P("dp", None),
        ),
        check_vma=False,
    )
```
